512 devices in a mesh: tgt: 16 (over z, x_lo), sup: 32 (over y, x_hi, core).
Axes of the slice: x: 4 (x_hi: 2, x_lo: 2; x = x_hi * 2 + x_lo), y: 8, z: 8, core: 2. Of those that a mesh axis runs over, the one named last changes fastest.
Arguments:
- cross_kernel: bfloat16 [32, 32, 512, 512], P('tgt', 'sup'), may hold values from -6 to 6
- cotangent: bfloat16 [32, 32, 512, 512], P('tgt', 'sup'), may hold values from -6 to 6
- self_tgt: bfloat16 [32, 512, 512], P('tgt', 'sup'), may hold values from -320 to 320
- self_sup: bfloat16 [32, 512, 512], P('sup', 'tgt'), may hold values from -320 to 320
Outputs:
- kernel_out: bfloat16 [32, 32, 512, 512], P('tgt', 'sup')
- grad_cross: bfloat16 [32, 32, 512, 512], P('tgt', 'sup')
- grad_self_tgt: float32 [32, 512, 512], P('tgt', 'sup')
- grad_self_sup: float32 [32, 512, 512], P('sup', 'tgt')
The draws below stay inside these ranges and needn't reach their ends.
All inputs are finite; a program needn't handle non-finite values.
Results may differ from the reference program's by a relative error of at most 0.02.
Values may be sent and summed in bfloat16 or wider, within the bound.
A program may use at most 64 MiB of HBM per device.

```python
import jax
import jax.numpy as jnp
from jax import lax

L = 512
TGT = 32
SUP = 32


def quiet_tokens(base_key, salt, doc_count):
    marks = jax.random.randint(jax.random.fold_in(jax.random.fold_in(base_key, salt), 99), (doc_count, L), 0, 2)
    return marks.astype(jnp.float32)


def draw_self(base_key, salt, doc_count):
    seeds = jax.random.split(jax.random.fold_in(base_key, salt), 6)
    quiet = quiet_tokens(base_key, salt, doc_count)[:, None, :]
    offset = jax.random.uniform(seeds[5], (doc_count, L, 1), jnp.float32, 2.0, 4.5)
    noise = jnp.clip(jax.random.normal(seeds[0], (doc_count, L, L), jnp.float32) * 0.3, -2.0, 2.0)
    scores = noise - offset * quiet
    return scores.astype(jnp.bfloat16)


def draw_self_tgt(key, part):
    return draw_self(key, 11, TGT)


def draw_self_sup(key, part):
    return draw_self(key, 23, SUP)


def draw_cross_kernel(key, part):
    quiet_tgt = quiet_tokens(key, 11, TGT)[:, None, :, None]
    quiet_sup = quiet_tokens(key, 23, SUP)[None, :, None, :]
    factor = 1.0 + 3.0 * jnp.maximum(quiet_tgt, quiet_sup)
    base = jax.random.normal(jax.random.fold_in(key, 37), (TGT, SUP, L, L), jnp.float32) * 0.5
    return jnp.clip(base * factor, -6.0, 6.0).astype(jnp.bfloat16)


def raised(result, rng, source, target, parts, factor):
    def block_of(dim):
        return (jnp.arange(result.shape[dim]) // (result.shape[dim] // parts)).reshape((-1,) + (1,) * (result.ndim - 1 - dim))

    first = jax.random.permutation(rng, parts)[block_of(target)]
    other_side = (block_of(target) + parts // 2) % parts
    return jnp.where((block_of(source) == first) | (block_of(source) == other_side), factor * result, result)


def shard_levels(own_key, dims, shards, low, top_value):
    gain, own = 1.0, jax.random.fold_in(own_key, 6)
    for axis_at, shards_of in shards:
        steps = jnp.exp(jax.random.uniform(jax.random.fold_in(own, axis_at), (shards_of,), jnp.float32, low / len(shards), top_value / len(shards)))
        gain = gain * jnp.repeat(steps, dims[axis_at] // shards_of).reshape([-1 if axis == axis_at else 1 for axis in range(len(dims))])
    return gain


def noise_with(key, dims, scale, bound, cuts, heavy, dtype=jnp.bfloat16):
    entries = scale * jax.random.normal(key, dims, jnp.float32)
    if cuts:
        entries = entries * shard_levels(key, dims, cuts, -0.22, 0.18)
    return jnp.clip(raised(entries, jax.random.fold_in(key, 3), *heavy), -bound, bound).astype(dtype)


def setup_inputs(seed: int = 0) -> dict:
    key_of = jax.random.split(jax.random.key(seed), 5)
    cross_kernel = draw_cross_kernel(jax.random.fold_in(key_of[4], 71), 0)
    cotangent = noise_with(key_of[1], (TGT, SUP, L, L), 1.0, 6.0, ((0, 16), (1, 32)), (1, 2, 32, 2.75))
    self_tgt = draw_self_tgt(jax.random.fold_in(key_of[4], 71), 0)
    self_sup = draw_self_sup(jax.random.fold_in(key_of[4], 71), 0)
    return {"cross_kernel": cross_kernel, "cotangent": cotangent, "self_tgt": self_tgt, "self_sup": self_sup}


def softmax_rows(scores):
    return jax.nn.softmax(scores.astype(jnp.float32), axis=-1).astype(jnp.bfloat16)


def soft_back(probs, dprobs):
    weights = probs.astype(jnp.float32)
    return weights * (dprobs - jnp.sum(dprobs * weights, axis=-1, keepdims=True))


def reference(cross_kernel, cotangent, self_tgt, self_sup):
    probs_sup = softmax_rows(self_sup)
    probs_tgt = softmax_rows(self_tgt)
    sup_float = probs_sup.astype(jnp.float32)

    def one_target(totals, inputs):
        kernel_tile, cot_tile, prob_tile = inputs
        kernel_f = kernel_tile.astype(jnp.float32)
        cot_f = cot_tile.astype(jnp.float32)
        prob_f = prob_tile.astype(jnp.float32)
        mixture = jnp.einsum('skl,sjl->skj', kernel_f, sup_float).astype(jnp.bfloat16)
        kernel_out = jnp.einsum('ik,skj->sij', prob_f, mixture.astype(jnp.float32)).astype(jnp.bfloat16)
        left_side = jnp.einsum('ik,skl->sil', prob_f, kernel_f).astype(jnp.bfloat16)
        held_grad = jnp.einsum('sik,skl->sil', cot_f, sup_float).astype(jnp.bfloat16)
        grad_cross = jnp.einsum('ki,skl->sil', prob_f, held_grad.astype(jnp.float32)).astype(jnp.bfloat16)
        dprob_tgt = jnp.einsum('sik,sjk->ij', cot_f, mixture.astype(jnp.float32))
        totals = totals + jnp.einsum('sij,sil->sjl', cot_f, left_side.astype(jnp.float32))
        grad_tgt = soft_back(prob_tile, dprob_tgt)
        return totals, (kernel_out, grad_cross, grad_tgt)

    start_sums = jnp.zeros((SUP, L, L), jnp.float32)
    totals, (kernel_out, grad_cross, grad_self_tgt) = lax.scan(
        one_target, start_sums, (cross_kernel, cotangent, probs_tgt))
    grad_self_sup = soft_back(probs_sup, totals)
    return kernel_out, grad_cross, grad_self_tgt, grad_self_sup
```

```python
import jax
import jax.numpy as jnp
from jax import lax
from jax.experimental import pallas as pl
from jax.experimental.pallas import tpu as pltpu
from jax.sharding import PartitionSpec as P

MESH = pl.DeviceIdType.MESH
F32 = jnp.float32
BF16 = jnp.bfloat16
L = 512
RING = 8


def softmax_rows(scores):
    scores = scores.astype(F32)
    e = jnp.exp(scores - jnp.max(scores, axis=-1, keepdims=True))
    return (e / jnp.sum(e, axis=-1, keepdims=True)).astype(BF16)


def soft_back(probs, dprobs):
    weights = probs.astype(F32)
    return weights * (dprobs - jnp.sum(dprobs * weights, axis=-1, keepdims=True))


def nn(a, b):
    return lax.dot_general(a, b, (((1,), (0,)), ((), ())), preferred_element_type=F32)


def nt(a, b):
    return lax.dot_general(a, b, (((1,), (1,)), ((), ())), preferred_element_type=F32)


def tn(a, b):
    return lax.dot_general(a, b, (((0,), (0,)), ((), ())), preferred_element_type=F32)


def hops(chunk, sign):
    return 4 if (chunk == 0) == (sign == 1) else 3


def kernel(
    cross_hbm, cot_hbm, tgt_ref, sup_ref,
    out_hbm, gcross_hbm, gtgt_ref, gsup_ref,
    cross, cot, pbuf, qbuf, mix, held, left, outv, gcv,
    dpart, dcore, epart, dstage, drecv, estage, erecv, dlast, elast,
    load_sem, store_sem,
    px_s, px_r, qx_s, qx_r, pr_s, pr_r, qr_s, qr_r, pc_s, pc_r,
    dc_s, dc_r, dr_s, dr_r, er_s, er_r, dx_s, dx_r, ex_s, ex_r,
):
    t_id = lax.axis_index("tgt")
    s_id = lax.axis_index("sup")
    z, x_lo = t_id // 2, t_id % 2
    y, x_hi, core = s_id // 4, (s_id // 2) % 2, s_id % 2

    def at_y(dy, xh=None, c=None):
        xh = x_hi if xh is None else xh
        c = core if c is None else c
        return (t_id, ((y + dy + RING) % RING) * 4 + xh * 2 + c)

    def at_z(dz, xl=None):
        xl = x_lo if xl is None else xl
        return (((z + dz + RING) % RING) * 2 + xl, s_id)

    loads = [
        pltpu.make_async_copy(cross_hbm, cross, load_sem.at[0]),
        pltpu.make_async_copy(cot_hbm, cot, load_sem.at[1]),
    ]
    for c in loads:
        c.start()

    barrier = pltpu.get_barrier_semaphore()
    near = [at_y(1), at_y(-1), at_y(0, xh=1 - x_hi), at_y(0, c=1 - core), at_z(1), at_z(-1), at_z(0, xl=1 - x_lo)]
    for device in near:
        pl.semaphore_signal(barrier, inc=1, device_id=device, device_id_type=MESH)

    p_own = softmax_rows(tgt_ref[...])
    q_own = softmax_rows(sup_ref[0])
    pbuf[s_id] = p_own
    qbuf[t_id] = q_own
    pl.semaphore_wait(barrier, 7)

    pending = []

    def send(src, dst, ssem, rsem, device):
        copy = pltpu.make_async_remote_copy(
            src_ref=src, dst_ref=dst, send_sem=ssem, recv_sem=rsem, device_id=device, device_id_type=MESH
        )
        copy.start()
        pending.append(copy)
        return copy

    def p_slot(dy, chunk):
        xh = x_hi if chunk == 0 else 1 - x_hi
        return ((y + dy + RING) % RING) * 4 + xh * 2 + core

    def q_slot(dz, chunk):
        xl = x_lo if chunk == 0 else 1 - x_lo
        return ((z + dz + RING) % RING) * 2 + xl

    def sems(ssem, rsem, chunk, sign, k):
        i = (chunk * 2 + (sign == 1)) * 4 + k
        return ssem.at[i], rsem.at[i]

    p_copies, q_copies, c_copies = {}, {}, []

    def q_ring(chunk, sign, k):
        slot = q_slot(-sign * k, chunk)
        ss, rs = sems(qr_s, qr_r, chunk, sign, k)
        q_copies[chunk, sign, k] = send(qbuf.at[slot], qbuf.at[slot], ss, rs, at_z(sign))

    def p_ring(chunk, sign, k):
        slot = p_slot(-sign * k, chunk)
        ss, rs = sems(pr_s, pr_r, chunk, sign, k)
        p_copies[chunk, sign, k] = send(pbuf.at[slot], pbuf.at[slot], ss, rs, at_y(sign))

    def p_core(dy, chunk):
        slot = p_slot(dy, chunk)
        i = len(c_copies)
        c_copies.append(send(pbuf.at[slot], pbuf.at[slot], pc_s.at[i], pc_r.at[i], at_y(0, c=1 - core)))

    qx = send(qbuf.at[t_id], qbuf.at[t_id], qx_s, qx_r, at_z(0, xl=1 - x_lo))
    px = send(pbuf.at[s_id], pbuf.at[s_id], px_s, px_r, at_y(0, xh=1 - x_hi))
    for sign in (1, -1):
        q_ring(0, sign, 0)
        p_ring(0, sign, 0)
    p_core(0, 0)

    for c in loads:
        c.wait()

    qx.wait_recv()
    for sign in (1, -1):
        q_ring(1, sign, 0)
    px.wait_recv()
    for sign in (1, -1):
        p_ring(1, sign, 0)
    p_core(0, 1)

    for k in range(4):
        for chunk in (0, 1):
            for sign in (1, -1):
                if k < hops(chunk, sign):
                    q_copies[chunk, sign, k].wait_recv()
                    if k + 1 < hops(chunk, sign):
                        q_ring(chunk, sign, k + 1)
            for sign in (1, -1):
                if k < hops(chunk, sign):
                    p_copies[chunk, sign, k].wait_recv()
                    if k + 1 < hops(chunk, sign):
                        p_ring(chunk, sign, k + 1)
                    p_core(-sign * (k + 1), chunk)

    q_all = qbuf[...].reshape(L, L)
    for t in range(2):
        mix[t] = nt(cross[t, 0], q_all).astype(BF16)
    for t in range(2):
        d = nt(cot[t, 0], mix[t]).astype(BF16)
        for s in range(32):
            dpart[s % 2, s // 4, (s // 2) % 2, t] = d[s * 16:(s + 1) * 16]

    order = (4, -3, 3, -2, 2, -1, 1, 0)
    d_core = {}
    for i, dy in enumerate(order):
        dest = (y + dy + RING) % RING
        d_core[dy % RING] = send(
            dpart.at[1 - core, dest], dcore.at[dest], dc_s.at[i], dc_r.at[i], at_y(0, c=1 - core)
        )

    for c in c_copies:
        c.wait_recv()
    for t in range(2):
        p_t = pbuf[:, t].reshape(L, L)
        left[t] = nn(p_t, cross[t, 0]).astype(BF16)
    e = tn(cot[0, 0], left[0]) + tn(cot[1, 0], left[1])
    epart[...] = e.astype(BF16).reshape(16, 32, L)

    def d_local(dy, chunk):
        dest = (y + dy + RING) % RING
        xh = x_hi if chunk == 0 else 1 - x_hi
        if dy % RING in d_core:
            d_core.pop(dy % RING).wait_recv()
        return dpart[core, dest, xh].astype(F32) + dcore[dest, xh].astype(F32)

    def e_local(dz, chunk):
        return epart[q_slot(dz, chunk)].astype(F32)

    d_copies, e_copies = {}, {}

    def d_ring(chunk, sign, k):
        n = hops(chunk, sign)
        i = (chunk * 2 + (sign == 1)) * 4 + k
        total = d_local(sign * (n - k), chunk)
        if k:
            total += drecv[i - 1].astype(F32)
        dstage[i] = total.astype(BF16)
        d_copies[chunk, sign, k] = send(dstage.at[i], drecv.at[i], dr_s.at[i], dr_r.at[i], at_y(sign))

    def e_ring(chunk, sign, k):
        n = hops(chunk, sign)
        i = (chunk * 2 + (sign == 1)) * 4 + k
        total = e_local(sign * (n - k), chunk)
        if k:
            total += erecv[i - 1].astype(F32)
        estage[i] = total.astype(BF16)
        e_copies[chunk, sign, k] = send(estage.at[i], erecv.at[i], er_s.at[i], er_r.at[i], at_z(sign))

    stores = []

    def work(i):
        t = i % 2
        if i < 2:
            outv[t, 0] = nn(pbuf[:, t].reshape(L, L), mix[t]).astype(BF16)
            stores.append(pltpu.make_async_copy(outv.at[t], out_hbm.at[t], store_sem.at[t]))
            stores[-1].start()
        elif i < 4:
            held[t] = nn(cot[t, 0], qbuf[...].reshape(L, L)).astype(BF16)
        elif i < 6:
            gcv[t, 0] = tn(pbuf[:, t].reshape(L, L), held[t]).astype(BF16)
            stores.append(pltpu.make_async_copy(gcv.at[t], gcross_hbm.at[t], store_sem.at[2 + t]))
            stores[-1].start()

    for k in range(4):
        for chunk in (1, 0):
            for sign in (1, -1):
                if k < hops(chunk, sign):
                    if k:
                        d_copies[chunk, sign, k - 1].wait_recv()
                    d_ring(chunk, sign, k)
            for sign in (1, -1):
                if k < hops(chunk, sign):
                    if k:
                        e_copies[chunk, sign, k - 1].wait_recv()
                    e_ring(chunk, sign, k)
        work(2 * k)
        work(2 * k + 1)

    def d_final(chunk):
        total = d_local(0, chunk)
        for sign in (1, -1):
            n = hops(chunk, sign)
            d_copies[chunk, sign, n - 1].wait_recv()
            total += drecv[(chunk * 2 + (sign == 1)) * 4 + n - 1].astype(F32)
        return total

    def e_final(chunk):
        total = e_local(0, chunk)
        for sign in (1, -1):
            n = hops(chunk, sign)
            e_copies[chunk, sign, n - 1].wait_recv()
            total += erecv[(chunk * 2 + (sign == 1)) * 4 + n - 1].astype(F32)
        return total

    dlast[0] = d_final(1).astype(BF16)
    dx = send(dlast.at[0], dlast.at[1], dx_s, dx_r, at_y(0, xh=1 - x_hi))
    elast[0] = e_final(1).astype(BF16)
    ex = send(elast.at[0], elast.at[1], ex_s, ex_r, at_z(0, xl=1 - x_lo))
    d_own = d_final(0)
    e_own = e_final(0)
    ex.wait_recv()
    gsup_ref[0] = soft_back(qbuf[t_id], e_own + elast[1].astype(F32))
    dx.wait_recv()
    gtgt_ref[...] = soft_back(pbuf[s_id], d_own + dlast[1].astype(F32))

    for copy in pending:
        copy.wait_send()
    for copy in stores:
        copy.wait()


def body(cross_kernel, cotangent, self_tgt, self_sup):
    vmem, dma = pltpu.VMEM, pltpu.SemaphoreType.DMA
    any_spec = pl.BlockSpec(memory_space=pl.ANY)
    vmem_spec = pl.BlockSpec(memory_space=pltpu.VMEM)
    docs = (2, 1, L, L)
    return pl.pallas_call(
        kernel,
        out_shape=(
            jax.ShapeDtypeStruct(docs, BF16),
            jax.ShapeDtypeStruct(docs, BF16),
            jax.ShapeDtypeStruct((2, 16, L), F32),
            jax.ShapeDtypeStruct((1, 32, L), F32),
        ),
        in_specs=[any_spec, any_spec, vmem_spec, vmem_spec],
        out_specs=(any_spec, any_spec, vmem_spec, vmem_spec),
        scratch_shapes=[
            vmem(docs, BF16), vmem(docs, BF16),
            vmem((32, 2, 16, L), BF16), vmem((16, 32, L), BF16),
            vmem((2, L, L), BF16), vmem((2, L, L), BF16), vmem((2, L, L), BF16),
            vmem(docs, BF16), vmem(docs, BF16),
            vmem((2, 8, 2, 2, 16, L), BF16), vmem((8, 2, 2, 16, L), BF16), vmem((16, 32, L), BF16),
            vmem((16, 2, 16, L), BF16), vmem((16, 2, 16, L), BF16),
            vmem((16, 32, L), BF16), vmem((16, 32, L), BF16),
            vmem((2, 2, 16, L), BF16), vmem((2, 32, L), BF16),
            dma((2,)), dma((4,)),
            dma, dma, dma, dma, dma((16,)), dma((16,)), dma((16,)), dma((16,)), dma((16,)), dma((16,)),
            dma((8,)), dma((8,)), dma((16,)), dma((16,)), dma((16,)), dma((16,)), dma, dma, dma, dma,
        ],
        compiler_params=pltpu.CompilerParams(
            collective_id=0, has_side_effects=True, vmem_limit_bytes=48 * 1024 * 1024
        ),
        name="layer",
    )(cross_kernel, cotangent, self_tgt, self_sup)


def solution(mesh):
    in_specs = (
        P("tgt", "sup", None, None),
        P("tgt", "sup", None, None),
        P("tgt", "sup", None),
        P("sup", "tgt", None),
    )
    out_specs = (
        P("tgt", "sup", None, None),
        P("tgt", "sup", None, None),
        P("tgt", "sup", None),
        P("sup", "tgt", None),
    )
    return jax.shard_map(body, mesh=mesh, in_specs=in_specs, out_specs=out_specs, check_vma=False)
```

```python
import jax
import jax.numpy as jnp
from jax import lax
from jax.experimental import pallas as pl
from jax.experimental.pallas import tpu as pltpu
from jax.sharding import PartitionSpec as P

MESH = pl.DeviceIdType.MESH
F32 = jnp.float32
BF16 = jnp.bfloat16
L = 512
RING = 8


def softmax_rows(scores):
    scores = scores.astype(F32)
    e = jnp.exp(scores - jnp.max(scores, axis=-1, keepdims=True))
    return (e / jnp.sum(e, axis=-1, keepdims=True)).astype(BF16)


def soft_back(probs, dprobs):
    weights = probs.astype(F32)
    return weights * (dprobs - jnp.sum(dprobs * weights, axis=-1, keepdims=True))


def nn(a, b):
    return lax.dot_general(a, b, (((1,), (0,)), ((), ())), preferred_element_type=F32)


def nt(a, b):
    return lax.dot_general(a, b, (((1,), (1,)), ((), ())), preferred_element_type=F32)


def tn(a, b):
    return lax.dot_general(a, b, (((0,), (0,)), ((), ())), preferred_element_type=F32)


def hops(chunk, sign):
    return 4 if (chunk == 0) == (sign == 1) else 3


def kernel(
    cross_hbm, cot_hbm, tgt_hbm, sup_hbm,
    outv, gcv, gtgt_ref, gsup_ref,
    cross, cot, tgt_ref, sup_ref, pbuf, qbuf, mix, held, left,
    dpart, dcore, epart, dstage, drecv, estage, erecv, dlast, elast,
    load_sem,
    px_s, px_r, qx_s, qx_r, pr_s, pr_r, qr_s, qr_r, pc_s, pc_r,
    dc_s, dc_r, dr_s, dr_r, er_s, er_r, dx_s, dx_r, ex_s, ex_r,
):
    t_id = lax.axis_index("tgt")
    s_id = lax.axis_index("sup")
    z, x_lo = t_id // 2, t_id % 2
    y, x_hi, core = s_id // 4, (s_id // 2) % 2, s_id % 2

    def at_y(dy, xh=None, c=None):
        xh = x_hi if xh is None else xh
        c = core if c is None else c
        return (t_id, ((y + dy + RING) % RING) * 4 + xh * 2 + c)

    def at_z(dz, xl=None):
        xl = x_lo if xl is None else xl
        return (((z + dz + RING) % RING) * 2 + xl, s_id)

    loads = [
        pltpu.make_async_copy(tgt_hbm, tgt_ref, load_sem.at[2]),
        pltpu.make_async_copy(sup_hbm, sup_ref, load_sem.at[3]),
        pltpu.make_async_copy(cross_hbm, cross, load_sem.at[0]),
        pltpu.make_async_copy(cot_hbm, cot, load_sem.at[1]),
    ]
    for c in loads:
        c.start()

    barrier = pltpu.get_barrier_semaphore()
    near = [at_y(1), at_y(-1), at_y(0, xh=1 - x_hi), at_y(0, c=1 - core), at_z(1), at_z(-1), at_z(0, xl=1 - x_lo)]
    for device in near:
        pl.semaphore_signal(barrier, inc=1, device_id=device, device_id_type=MESH)

    loads.pop(0).wait()
    loads.pop(0).wait()
    p_own = softmax_rows(tgt_ref[...])
    q_own = softmax_rows(sup_ref[0])
    pbuf[s_id] = p_own
    qbuf[t_id] = q_own
    pl.semaphore_wait(barrier, 7)

    pending = []

    def send(src, dst, ssem, rsem, device):
        copy = pltpu.make_async_remote_copy(
            src_ref=src, dst_ref=dst, send_sem=ssem, recv_sem=rsem, device_id=device, device_id_type=MESH
        )
        copy.start()
        pending.append(copy)
        return copy

    def p_slot(dy, chunk):
        xh = x_hi if chunk == 0 else 1 - x_hi
        return ((y + dy + RING) % RING) * 4 + xh * 2 + core

    def q_slot(dz, chunk):
        xl = x_lo if chunk == 0 else 1 - x_lo
        return ((z + dz + RING) % RING) * 2 + xl

    def sems(ssem, rsem, chunk, sign, k):
        i = (chunk * 2 + (sign == 1)) * 4 + k
        return ssem.at[i], rsem.at[i]

    p_copies, q_copies, c_copies = {}, {}, []

    def q_ring(chunk, sign, k):
        slot = q_slot(-sign * k, chunk)
        ss, rs = sems(qr_s, qr_r, chunk, sign, k)
        q_copies[chunk, sign, k] = send(qbuf.at[slot], qbuf.at[slot], ss, rs, at_z(sign))

    def p_ring(chunk, sign, k):
        slot = p_slot(-sign * k, chunk)
        ss, rs = sems(pr_s, pr_r, chunk, sign, k)
        p_copies[chunk, sign, k] = send(pbuf.at[slot], pbuf.at[slot], ss, rs, at_y(sign))

    def p_core(dy, chunk):
        slot = p_slot(dy, chunk)
        i = len(c_copies)
        c_copies.append(send(pbuf.at[slot], pbuf.at[slot], pc_s.at[i], pc_r.at[i], at_y(0, c=1 - core)))

    qx = send(qbuf.at[t_id], qbuf.at[t_id], qx_s, qx_r, at_z(0, xl=1 - x_lo))
    px = send(pbuf.at[s_id], pbuf.at[s_id], px_s, px_r, at_y(0, xh=1 - x_hi))
    for sign in (1, -1):
        q_ring(0, sign, 0)
        p_ring(0, sign, 0)
    p_core(0, 0)

    for c in loads:
        c.wait()

    qx.wait_recv()
    for sign in (1, -1):
        q_ring(1, sign, 0)
    px.wait_recv()
    for sign in (1, -1):
        p_ring(1, sign, 0)
    p_core(0, 1)

    for k in range(4):
        for chunk in (0, 1):
            for sign in (1, -1):
                if k < hops(chunk, sign):
                    q_copies[chunk, sign, k].wait_recv()
                    if k + 1 < hops(chunk, sign):
                        q_ring(chunk, sign, k + 1)
            for sign in (1, -1):
                if k < hops(chunk, sign):
                    p_copies[chunk, sign, k].wait_recv()
                    if k + 1 < hops(chunk, sign):
                        p_ring(chunk, sign, k + 1)
                    p_core(-sign * (k + 1), chunk)

    q_all = qbuf[...].reshape(L, L)
    for t in range(2):
        mix[t] = nt(cross[t, 0], q_all).astype(BF16)
    for t in range(2):
        d = nt(cot[t, 0], mix[t]).astype(BF16)
        for s in range(32):
            dpart[s % 2, s // 4, (s // 2) % 2, t] = d[s * 16:(s + 1) * 16]

    order = (4, -3, 3, -2, 2, -1, 1, 0)
    d_core = {}
    for i, dy in enumerate(order):
        dest = (y + dy + RING) % RING
        d_core[dy % RING] = send(
            dpart.at[1 - core, dest], dcore.at[dest], dc_s.at[i], dc_r.at[i], at_y(0, c=1 - core)
        )

    for c in c_copies:
        c.wait_recv()
    for t in range(2):
        p_t = pbuf[:, t].reshape(L, L)
        left[t] = nn(p_t, cross[t, 0]).astype(BF16)
    e = tn(cot[0, 0], left[0]) + tn(cot[1, 0], left[1])
    epart[...] = e.astype(BF16).reshape(16, 32, L)

    def d_local(dy, chunk):
        dest = (y + dy + RING) % RING
        xh = x_hi if chunk == 0 else 1 - x_hi
        if dy % RING in d_core:
            d_core.pop(dy % RING).wait_recv()
        return dpart[core, dest, xh].astype(F32) + dcore[dest, xh].astype(F32)

    def e_local(dz, chunk):
        return epart[q_slot(dz, chunk)].astype(F32)

    d_copies, e_copies = {}, {}

    def d_ring(chunk, sign, k):
        n = hops(chunk, sign)
        i = (chunk * 2 + (sign == 1)) * 4 + k
        total = d_local(sign * (n - k), chunk)
        if k:
            total += drecv[i - 1].astype(F32)
        dstage[i] = total.astype(BF16)
        d_copies[chunk, sign, k] = send(dstage.at[i], drecv.at[i], dr_s.at[i], dr_r.at[i], at_y(sign))

    def e_ring(chunk, sign, k):
        n = hops(chunk, sign)
        i = (chunk * 2 + (sign == 1)) * 4 + k
        total = e_local(sign * (n - k), chunk)
        if k:
            total += erecv[i - 1].astype(F32)
        estage[i] = total.astype(BF16)
        e_copies[chunk, sign, k] = send(estage.at[i], erecv.at[i], er_s.at[i], er_r.at[i], at_z(sign))

    def work(i):
        t = i % 2
        if i < 2:
            outv[t, 0] = nn(pbuf[:, t].reshape(L, L), mix[t]).astype(BF16)
        elif i < 4:
            held[t] = nn(cot[t, 0], qbuf[...].reshape(L, L)).astype(BF16)
        elif i < 6:
            gcv[t, 0] = tn(pbuf[:, t].reshape(L, L), held[t]).astype(BF16)

    for k in range(4):
        for chunk in (1, 0):
            for sign in (1, -1):
                if k < hops(chunk, sign):
                    if k:
                        d_copies[chunk, sign, k - 1].wait_recv()
                    d_ring(chunk, sign, k)
            for sign in (1, -1):
                if k < hops(chunk, sign):
                    if k:
                        e_copies[chunk, sign, k - 1].wait_recv()
                    e_ring(chunk, sign, k)
        work(2 * k)
        work(2 * k + 1)

    def d_final(chunk):
        total = d_local(0, chunk)
        for sign in (1, -1):
            n = hops(chunk, sign)
            d_copies[chunk, sign, n - 1].wait_recv()
            total += drecv[(chunk * 2 + (sign == 1)) * 4 + n - 1].astype(F32)
        return total

    def e_final(chunk):
        total = e_local(0, chunk)
        for sign in (1, -1):
            n = hops(chunk, sign)
            e_copies[chunk, sign, n - 1].wait_recv()
            total += erecv[(chunk * 2 + (sign == 1)) * 4 + n - 1].astype(F32)
        return total

    dlast[0] = d_final(1).astype(BF16)
    dx = send(dlast.at[0], dlast.at[1], dx_s, dx_r, at_y(0, xh=1 - x_hi))
    elast[0] = e_final(1).astype(BF16)
    ex = send(elast.at[0], elast.at[1], ex_s, ex_r, at_z(0, xl=1 - x_lo))
    d_own = d_final(0)
    e_own = e_final(0)
    ex.wait_recv()
    gsup_ref[0] = soft_back(qbuf[t_id], e_own + elast[1].astype(F32))
    dx.wait_recv()
    gtgt_ref[...] = soft_back(pbuf[s_id], d_own + dlast[1].astype(F32))

    for copy in pending:
        copy.wait_send()


def write_out(*refs):
    copies = [pltpu.make_async_copy(refs[i], refs[4 + i], refs[8].at[i]) for i in range(4)]
    for copy in copies:
        copy.start()
    for copy in copies:
        copy.wait()


def body(cross_kernel, cotangent, self_tgt, self_sup):
    vmem, dma = pltpu.VMEM, pltpu.SemaphoreType.DMA
    hbm_spec = pl.BlockSpec(memory_space=pltpu.HBM)
    vmem_spec = pl.BlockSpec(memory_space=pltpu.VMEM)
    docs = (2, 1, L, L)
    outs = (
        jax.ShapeDtypeStruct(docs, BF16),
        jax.ShapeDtypeStruct(docs, BF16),
        jax.ShapeDtypeStruct((2, 16, L), F32),
        jax.ShapeDtypeStruct((1, 32, L), F32),
    )
    results = pl.pallas_call(
        kernel,
        out_shape=outs,
        in_specs=[hbm_spec] * 4,
        out_specs=(vmem_spec,) * 4,
        scratch_shapes=[
            vmem(docs, BF16), vmem(docs, BF16), vmem((2, 16, L), BF16), vmem((1, 32, L), BF16),
            vmem((32, 2, 16, L), BF16), vmem((16, 32, L), BF16),
            vmem((2, L, L), BF16), vmem((2, L, L), BF16), vmem((2, L, L), BF16),
            vmem((2, 8, 2, 2, 16, L), BF16), vmem((8, 2, 2, 16, L), BF16), vmem((16, 32, L), BF16),
            vmem((16, 2, 16, L), BF16), vmem((16, 2, 16, L), BF16),
            vmem((16, 32, L), BF16), vmem((16, 32, L), BF16),
            vmem((2, 2, 16, L), BF16), vmem((2, 32, L), BF16),
            dma((4,)),
            dma, dma, dma, dma, dma((16,)), dma((16,)), dma((16,)), dma((16,)), dma((16,)), dma((16,)),
            dma((8,)), dma((8,)), dma((16,)), dma((16,)), dma((16,)), dma((16,)), dma, dma, dma, dma,
        ],
        compiler_params=pltpu.CompilerParams(
            collective_id=0, has_side_effects=True, vmem_limit_bytes=48 * 1024 * 1024
        ),
        name="layer",
    )(*[pltpu.with_memory_space_constraint(x, pltpu.HBM) for x in (cross_kernel, cotangent, self_tgt, self_sup)])
    return pl.pallas_call(
        write_out,
        out_shape=outs,
        in_specs=[vmem_spec] * 4,
        out_specs=(hbm_spec,) * 4,
        scratch_shapes=[dma((4,))],
        compiler_params=pltpu.CompilerParams(vmem_limit_bytes=1024 * 1024),
        name="write_out",
    )(*results)


def solution(mesh):
    in_specs = (
        P("tgt", "sup", None, None),
        P("tgt", "sup", None, None),
        P("tgt", "sup", None),
        P("sup", "tgt", None),
    )
    out_specs = (
        P("tgt", "sup", None, None),
        P("tgt", "sup", None, None),
        P("tgt", "sup", None),
        P("sup", "tgt", None),
    )
    return jax.shard_map(body, mesh=mesh, in_specs=in_specs, out_specs=out_specs, check_vma=False)
```

```python
import jax
import jax.numpy as jnp
from jax import lax
from jax.experimental import pallas as pl
from jax.experimental.pallas import tpu as pltpu
from jax.sharding import PartitionSpec as P

MESH = pl.DeviceIdType.MESH
F32 = jnp.float32
BF16 = jnp.bfloat16
L = 512
RING = 8


def softmax_rows(scores):
    scores = scores.astype(F32)
    e = jnp.exp(scores - jnp.max(scores, axis=-1, keepdims=True))
    return (e / jnp.sum(e, axis=-1, keepdims=True)).astype(BF16)


def soft_back(probs, dprobs):
    weights = probs.astype(F32)
    return weights * (dprobs - jnp.sum(dprobs * weights, axis=-1, keepdims=True))


def nn(a, b):
    return lax.dot_general(a, b, (((1,), (0,)), ((), ())), preferred_element_type=F32)


def nt(a, b):
    return lax.dot_general(a, b, (((1,), (1,)), ((), ())), preferred_element_type=F32)


def tn(a, b):
    return lax.dot_general(a, b, (((0,), (0,)), ((), ())), preferred_element_type=F32)


def kernel(
    cross_hbm, cot_hbm, tgt_hbm, sup_hbm,
    outv, gcv, gtgt_ref, gsup_ref,
    cross, cot, tgt_ref, sup_ref, pbuf, qbuf, mix, held, left,
    dpart, dcore, epart, ecross, dstage, drecv, estage, erecv, dlast,
    load_sem,
    px_s, px_r, qx_s, qx_r, pr_s, pr_r, qr_s, qr_r, pc_s, pc_r,
    dc_s, dc_r, dr_s, dr_r, er_s, er_r, dx_s, dx_r, ex_s, ex_r,
):
    t_id = lax.axis_index("tgt")
    s_id = lax.axis_index("sup")
    z, x_lo = t_id // 2, t_id % 2
    y, x_hi, core = s_id // 4, (s_id // 2) % 2, s_id % 2

    def at_y(dy, xh=None, c=None):
        xh = x_hi if xh is None else xh
        c = core if c is None else c
        return (t_id, ((y + dy + RING) % RING) * 4 + xh * 2 + c)

    def at_z(dz, xl=None):
        xl = x_lo if xl is None else xl
        return (((z + dz + RING) % RING) * 2 + xl, s_id)

    loads = [
        pltpu.make_async_copy(tgt_hbm, tgt_ref, load_sem.at[2]),
        pltpu.make_async_copy(sup_hbm, sup_ref, load_sem.at[3]),
        pltpu.make_async_copy(cross_hbm, cross, load_sem.at[0]),
        pltpu.make_async_copy(cot_hbm, cot, load_sem.at[1]),
    ]
    for c in loads:
        c.start()

    barrier = pltpu.get_barrier_semaphore()
    near = [at_y(0, xh=1 - x_hi), at_y(0, c=1 - core), at_z(0, xl=1 - x_lo)]
    near += [at(step) for at in (at_y, at_z) for step in (2, -2, 1, -1)]
    for device in near:
        pl.semaphore_signal(barrier, inc=1, device_id=device, device_id_type=MESH)

    loads.pop(0).wait()
    loads.pop(0).wait()
    p_own = softmax_rows(tgt_ref[...])
    q_own = softmax_rows(sup_ref[0])
    pbuf[s_id] = p_own
    qbuf[t_id] = q_own
    pl.semaphore_wait(barrier, len(near))

    pending = []

    def send(src, dst, ssem, rsem, device):
        copy = pltpu.make_async_remote_copy(
            src_ref=src, dst_ref=dst, send_sem=ssem, recv_sem=rsem, device_id=device, device_id_type=MESH
        )
        copy.start()
        pending.append(copy)
        return copy

    def p_slot(dy, chunk):
        xh = x_hi if chunk == 0 else 1 - x_hi
        return ((y + dy + RING) % RING) * 4 + xh * 2 + core

    def q_slot(dz, chunk=0):
        xl = x_lo if chunk == 0 else 1 - x_lo
        return ((z + dz + RING) % RING) * 2 + xl

    def place(chunk, origin, half=0):
        return chunk * 9 + (origin + 3 if origin != 4 else 7 + half)

    c_copies = []

    def p_send(chunk, origin, step):
        slot = p_slot(origin, chunk)
        i = place(chunk, origin - step)
        return send(pbuf.at[slot], pbuf.at[slot], pr_s.at[i], pr_r.at[i], at_y(step))

    def p_half(chunk, sign):
        slot = p_slot(-2 * sign, chunk)
        h = (1 - sign) // 2
        i = place(chunk, 4, h)
        return send(pbuf.at[slot, h], pbuf.at[slot, h], pr_s.at[i], pr_r.at[i], at_y(2 * sign))

    def q_send(origin, step):
        slot = q_slot(origin)
        i = place(0, origin - step)
        return send(qbuf.at[slot], qbuf.at[slot], qr_s.at[i], qr_r.at[i], at_z(step))

    def q_half(sign):
        slot = q_slot(-2 * sign)
        h = (1 - sign) // 2
        i = place(0, 4, h)
        rows = pl.ds(h * 16, 16)
        return send(qbuf.at[slot, rows], qbuf.at[slot, rows], qr_s.at[i], qr_r.at[i], at_z(2 * sign))

    def q_cross(dz):
        slot = q_slot(dz)
        i = dz + 3
        return send(qbuf.at[slot], qbuf.at[slot], qx_s.at[i], qx_r.at[i], at_z(0, xl=1 - x_lo))

    def p_core(dy, chunk):
        slot = p_slot(dy, chunk)
        i = len(c_copies)
        c_copies.append(send(pbuf.at[slot], pbuf.at[slot], pc_s.at[i], pc_r.at[i], at_y(0, c=1 - core)))

    q_in, x_in, p_in = {}, [], {}
    for step in (2, -2, 1, -1):
        q_in[step] = q_send(0, step)
    x_in.append(q_cross(0))
    px = send(pbuf.at[s_id], pbuf.at[s_id], px_s, px_r, at_y(0, xh=1 - x_hi))
    for step in (2, -2, 1, -1):
        p_in[0, step] = p_send(0, 0, step)
    p_core(0, 0)

    for c in loads:
        c.wait()

    for sign in (1, -1):
        q_in[sign].wait_recv()
        x_in.append(q_cross(-sign))
    for sign in (1, -1):
        q_in[2 * sign].wait_recv()
        q_in[3 * sign] = q_send(-2 * sign, sign)
        q_in[4 * sign] = q_half(sign)
        x_in.append(q_cross(-2 * sign))
    for sign in (1, -1):
        p_in[0, sign].wait_recv()
        p_core(-sign, 0)

    def p_second(chunk):
        for sign in (1, -1):
            p_in[chunk, 2 * sign].wait_recv()
            p_in[chunk, 3 * sign] = p_send(chunk, -2 * sign, sign)
            p_in[chunk, 4 * sign] = p_half(chunk, sign)
            p_core(-2 * sign, chunk)

    def p_third(chunk):
        for sign in (1, -1):
            p_in[chunk, 3 * sign].wait_recv()
            p_core(-3 * sign, chunk)
        for sign in (1, -1):
            p_in[chunk, 4 * sign].wait_recv()
        p_core(4, chunk)

    p_second(0)
    px.wait_recv()
    for step in (2, -2, 1, -1):
        p_in[1, step] = p_send(1, 0, step)
    p_core(0, 1)
    for sign in (1, -1):
        q_in[3 * sign].wait_recv()
        x_in.append(q_cross(-3 * sign))
    for sign in (1, -1):
        q_in[4 * sign].wait_recv()
    x_in.append(q_cross(4))
    p_third(0)
    for sign in (1, -1):
        p_in[1, sign].wait_recv()
        p_core(-sign, 1)
    p_second(1)

    for c in x_in:
        c.wait_recv()
    q_all = qbuf[...].reshape(L, L)
    for t in range(2):
        mix[t] = nt(cross[t, 0], q_all).astype(BF16)
    p_third(1)
    for t in range(2):
        d = nt(cot[t, 0], mix[t]).astype(BF16)
        for s in range(32):
            dpart[s % 2, s // 4, (s // 2) % 2, t] = d[s * 16:(s + 1) * 16]

    order = (4, 3, -3, 2, -2, 1, -1, 0)
    d_in = {}
    for i, dy in enumerate(order):
        dest = (y + dy + RING) % RING
        d_in[dy] = send(
            dpart.at[1 - core, dest], dcore.at[dest], dc_s.at[i], dc_r.at[i], at_y(0, c=1 - core)
        )

    for c in c_copies:
        c.wait_recv()
    for t in range(2):
        p_t = pbuf[:, t].reshape(L, L)
        left[t] = nn(p_t, cross[t, 0]).astype(BF16)
    e = tn(cot[0, 0], left[0]) + tn(cot[1, 0], left[1])
    epart[...] = e.astype(BF16).reshape(16, 32, L)

    e_in = {}
    for i, dz in enumerate(order):
        slot = q_slot(dz, 1)
        e_in[dz] = send(epart.at[slot], ecross.at[i], ex_s.at[i], ex_r.at[i], at_z(0, xl=1 - x_lo))

    def d_local(dy, chunk):
        dest = (y + dy + RING) % RING
        xh = x_hi if chunk == 0 else 1 - x_hi
        return dpart[core, dest, xh].astype(F32) + dcore[dest, xh].astype(F32)

    def e_local(dz):
        return epart[q_slot(dz)].astype(F32) + ecross[order.index(dz)].astype(F32)

    d_out, e_out = {}, {}

    def d_send(chunk, dy, step, value):
        i = place(chunk, dy)
        dstage[i] = value.astype(BF16)
        d_out[chunk, dy] = send(dstage.at[i], drecv.at[i], dr_s.at[i], dr_r.at[i], at_y(step))

    def d_half(chunk, sign):
        h = (1 - sign) // 2
        i, j = place(chunk, 4), place(chunk, 4, h)
        d_out[chunk, 4 * sign] = send(
            dstage.at[i, h], drecv.at[i, h], dr_s.at[j], dr_r.at[j], at_y(2 * sign)
        )

    def e_send(dz, step, value):
        i = place(0, dz)
        estage[i] = value.astype(BF16)
        e_out[dz] = send(estage.at[i], erecv.at[i], er_s.at[i], er_r.at[i], at_z(step))

    def e_half(sign):
        h = (1 - sign) // 2
        i, j = place(0, 4), place(0, 4, h)
        rows = pl.ds(h * 16, 16)
        e_out[4 * sign] = send(
            estage.at[i, rows], erecv.at[i, rows], er_s.at[j], er_r.at[j], at_z(2 * sign)
        )

    def d_first(chunk):
        dstage[place(chunk, 4)] = d_local(4, chunk).astype(BF16)
        for sign in (1, -1):
            d_half(chunk, sign)
        for sign in (1, -1):
            d_send(chunk, 3 * sign, sign, d_local(3 * sign, chunk))

    def d_second(chunk):
        for sign in (1, -1):
            d_out[chunk, 3 * sign].wait_recv()
            d_out[chunk, 4 * sign].wait_recv()
            h = (1 - sign) // 2
            total = d_local(2 * sign, chunk) + drecv[place(chunk, 3 * sign)].astype(F32)
            far = drecv[place(chunk, 4), h].astype(F32)
            both = [total[0], total[1]]
            both[h] = both[h] + far
            i = place(chunk, 2 * sign)
            dstage[i, 0] = both[0].astype(BF16)
            dstage[i, 1] = both[1].astype(BF16)
            d_out[chunk, 2 * sign] = send(dstage.at[i], drecv.at[i], dr_s.at[i], dr_r.at[i], at_y(2 * sign))

    def d_third(chunk):
        for sign in (1, -1):
            d_send(chunk, sign, sign, d_local(sign, chunk))

    def e_first():
        for dz in (4, 3, -3):
            e_in[dz].wait_recv()
        estage[place(0, 4)] = e_local(4).astype(BF16)
        for sign in (1, -1):
            e_half(sign)
        for sign in (1, -1):
            e_send(3 * sign, sign, e_local(3 * sign))

    def e_second():
        for dz in (2, -2):
            e_in[dz].wait_recv()
        for sign in (1, -1):
            e_out[3 * sign].wait_recv()
            e_out[4 * sign].wait_recv()
            h = (1 - sign) // 2
            total = e_local(2 * sign) + erecv[place(0, 3 * sign)].astype(F32)
            far = erecv[place(0, 4), h * 16:(h + 1) * 16].astype(F32)
            both = [total[:16], total[16:]]
            both[h] = both[h] + far
            i = place(0, 2 * sign)
            estage[i, 0:16] = both[0].astype(BF16)
            estage[i, 16:32] = both[1].astype(BF16)
            e_out[2 * sign] = send(estage.at[i], erecv.at[i], er_s.at[i], er_r.at[i], at_z(2 * sign))

    def e_third():
        for dz in (1, -1, 0):
            e_in[dz].wait_recv()
        for sign in (1, -1):
            e_send(sign, sign, e_local(sign))

    def out_part(t):
        outv[t, 0] = nn(pbuf[:, t].reshape(L, L), mix[t]).astype(BF16)

    def held_part(t):
        held[t] = nn(cot[t, 0], qbuf[...].reshape(L, L)).astype(BF16)

    def gcross_part(t):
        gcv[t, 0] = tn(pbuf[:, t].reshape(L, L), held[t]).astype(BF16)

    for dy in order:
        d_in[dy].wait_recv()
    d_first(1)
    d_first(0)
    d_third(1)
    e_first()
    held_part(0)
    held_part(1)
    d_second(1)
    e_second()
    e_third()
    d_second(0)
    d_third(0)
    out_part(0)
    out_part(1)
    gcross_part(0)
    gcross_part(1)

    def d_final(chunk):
        total = d_local(0, chunk)
        for step in (1, -1, 2, -2):
            d_out[chunk, step].wait_recv()
            total += drecv[place(chunk, step)].astype(F32)
        return total

    dlast[0] = d_final(1).astype(BF16)
    dx = send(dlast.at[0], dlast.at[1], dx_s, dx_r, at_y(0, xh=1 - x_hi))
    total = e_local(0)
    for step in (1, -1, 2, -2):
        e_out[step].wait_recv()
        total += erecv[place(0, step)].astype(F32)
    gsup_ref[0] = soft_back(qbuf[t_id], total)
    d_own = d_final(0)
    dx.wait_recv()
    gtgt_ref[...] = soft_back(pbuf[s_id], d_own + dlast[1].astype(F32))

    for copy in pending:
        copy.wait_send()


def write_out(*refs):
    copies = [pltpu.make_async_copy(refs[i], refs[4 + i], refs[8].at[i]) for i in range(4)]
    for copy in copies:
        copy.start()
    for copy in copies:
        copy.wait()


def body(cross_kernel, cotangent, self_tgt, self_sup):
    vmem, dma = pltpu.VMEM, pltpu.SemaphoreType.DMA
    hbm_spec = pl.BlockSpec(memory_space=pltpu.HBM)
    vmem_spec = pl.BlockSpec(memory_space=pltpu.VMEM)
    docs = (2, 1, L, L)
    outs = (
        jax.ShapeDtypeStruct(docs, BF16),
        jax.ShapeDtypeStruct(docs, BF16),
        jax.ShapeDtypeStruct((2, 16, L), F32),
        jax.ShapeDtypeStruct((1, 32, L), F32),
    )
    results = pl.pallas_call(
        kernel,
        out_shape=outs,
        in_specs=[hbm_spec] * 4,
        out_specs=(vmem_spec,) * 4,
        scratch_shapes=[
            vmem(docs, BF16), vmem(docs, BF16), vmem((2, 16, L), BF16), vmem((1, 32, L), BF16),
            vmem((32, 2, 16, L), BF16), vmem((16, 32, L), BF16),
            vmem((2, L, L), BF16), vmem((2, L, L), BF16), vmem((2, L, L), BF16),
            vmem((2, 8, 2, 2, 16, L), BF16), vmem((8, 2, 2, 16, L), BF16),
            vmem((16, 32, L), BF16), vmem((8, 32, L), BF16),
            vmem((18, 2, 16, L), BF16), vmem((18, 2, 16, L), BF16),
            vmem((9, 32, L), BF16), vmem((9, 32, L), BF16),
            vmem((2, 2, 16, L), BF16),
            dma((4,)),
            dma, dma, dma((8,)), dma((8,)), dma((18,)), dma((18,)), dma((9,)), dma((9,)), dma((16,)), dma((16,)),
            dma((8,)), dma((8,)), dma((18,)), dma((18,)), dma((9,)), dma((9,)), dma, dma, dma((8,)), dma((8,)),
        ],
        compiler_params=pltpu.CompilerParams(
            collective_id=0, has_side_effects=True, vmem_limit_bytes=48 * 1024 * 1024
        ),
        name="layer",
    )(*[pltpu.with_memory_space_constraint(x, pltpu.HBM) for x in (cross_kernel, cotangent, self_tgt, self_sup)])
    return pl.pallas_call(
        write_out,
        out_shape=outs,
        in_specs=[vmem_spec] * 4,
        out_specs=(hbm_spec,) * 4,
        scratch_shapes=[dma((4,))],
        compiler_params=pltpu.CompilerParams(vmem_limit_bytes=1024 * 1024),
        name="write_out",
    )(*results)


def solution(mesh):
    in_specs = (
        P("tgt", "sup", None, None),
        P("tgt", "sup", None, None),
        P("tgt", "sup", None),
        P("sup", "tgt", None),
    )
    out_specs = (
        P("tgt", "sup", None, None),
        P("tgt", "sup", None, None),
        P("tgt", "sup", None),
        P("sup", "tgt", None),
    )
    return jax.shard_map(body, mesh=mesh, in_specs=in_specs, out_specs=out_specs, check_vma=False)
```

```python
import jax
import jax.numpy as jnp
from jax import lax
from jax.experimental import pallas as pl
from jax.experimental.pallas import tpu as pltpu
from jax.sharding import PartitionSpec as P

MESH = pl.DeviceIdType.MESH
F32 = jnp.float32
BF16 = jnp.bfloat16
L = 512
RING = 8


def softmax_rows(scores):
    scores = scores.astype(F32)
    e = jnp.exp(scores - jnp.max(scores, axis=-1, keepdims=True))
    return (e / jnp.sum(e, axis=-1, keepdims=True)).astype(BF16)


def soft_back(probs, dprobs):
    weights = probs.astype(F32)
    return weights * (dprobs - jnp.sum(dprobs * weights, axis=-1, keepdims=True))


def nn(a, b):
    return lax.dot_general(a, b, (((1,), (0,)), ((), ())), preferred_element_type=F32)


def nt(a, b):
    return lax.dot_general(a, b, (((1,), (1,)), ((), ())), preferred_element_type=F32)


def tn(a, b):
    return lax.dot_general(a, b, (((0,), (0,)), ((), ())), preferred_element_type=F32)


def kernel(
    cross_hbm, cot_hbm, tgt_hbm, sup_hbm,
    outv, gcv, gtgt_ref, gsup_ref,
    cross, cot, tgt_ref, sup_ref, pbuf, qbuf, mix, held, left,
    dpart, dcore, epart, ecross, dstage, drecv, estage, erecv, dlast, dxs, dcross,
    load_sem,
    px_s, px_r, qx_s, qx_r, pr_s, pr_r, qr_s, qr_r, pc_s, pc_r,
    dc_s, dc_r, dr_s, dr_r, er_s, er_r, dx_s, dx_r, ex_s, ex_r,
):
    t_id = lax.axis_index("tgt")
    s_id = lax.axis_index("sup")
    z, x_lo = t_id // 2, t_id % 2
    y, x_hi, core = s_id // 4, (s_id // 2) % 2, s_id % 2

    def at_y(dy, xh=None, c=None):
        xh = x_hi if xh is None else xh
        c = core if c is None else c
        return (t_id, ((y + dy + RING) % RING) * 4 + xh * 2 + c)

    def at_z(dz, xl=None):
        xl = x_lo if xl is None else xl
        return (((z + dz + RING) % RING) * 2 + xl, s_id)

    loads = [
        pltpu.make_async_copy(tgt_hbm, tgt_ref, load_sem.at[2]),
        pltpu.make_async_copy(sup_hbm, sup_ref, load_sem.at[3]),
        pltpu.make_async_copy(cross_hbm, cross, load_sem.at[0]),
        pltpu.make_async_copy(cot_hbm, cot, load_sem.at[1]),
    ]
    for c in loads:
        c.start()

    barrier = pltpu.get_barrier_semaphore()
    near = [at_y(0, xh=1 - x_hi), at_y(0, c=1 - core), at_z(0, xl=1 - x_lo)]
    near += [at(step) for at in (at_y, at_z) for step in (2, -2, 1, -1)]
    for device in near:
        pl.semaphore_signal(barrier, inc=1, device_id=device, device_id_type=MESH)

    loads.pop(0).wait()
    loads.pop(0).wait()
    p_own = softmax_rows(tgt_ref[...])
    q_own = softmax_rows(sup_ref[0])
    pbuf[s_id] = p_own
    qbuf[t_id] = q_own
    pl.semaphore_wait(barrier, len(near))

    pending = []

    def send(src, dst, ssem, rsem, device):
        copy = pltpu.make_async_remote_copy(
            src_ref=src, dst_ref=dst, send_sem=ssem, recv_sem=rsem, device_id=device, device_id_type=MESH
        )
        copy.start()
        pending.append(copy)
        return copy

    def p_slot(dy, chunk):
        xh = x_hi if chunk == 0 else 1 - x_hi
        return ((y + dy + RING) % RING) * 4 + xh * 2 + core

    def q_slot(dz, chunk=0):
        xl = x_lo if chunk == 0 else 1 - x_lo
        return ((z + dz + RING) % RING) * 2 + xl

    def place(chunk, origin, half=0):
        return chunk * 9 + (origin + 3 if origin != 4 else 7 + half)

    c_copies = []

    def p_send(chunk, origin, step):
        slot = p_slot(origin, chunk)
        i = place(chunk, origin - step)
        return send(pbuf.at[slot], pbuf.at[slot], pr_s.at[i], pr_r.at[i], at_y(step))

    def p_half(chunk, sign):
        slot = p_slot(-2 * sign, chunk)
        h = (1 - sign) // 2
        i = place(chunk, 4, h)
        return send(pbuf.at[slot, h], pbuf.at[slot, h], pr_s.at[i], pr_r.at[i], at_y(2 * sign))

    def q_send(origin, step):
        slot = q_slot(origin)
        i = place(0, origin - step)
        return send(qbuf.at[slot], qbuf.at[slot], qr_s.at[i], qr_r.at[i], at_z(step))

    def q_half(sign):
        slot = q_slot(-2 * sign)
        h = (1 - sign) // 2
        i = place(0, 4, h)
        rows = pl.ds(h * 16, 16)
        return send(qbuf.at[slot, rows], qbuf.at[slot, rows], qr_s.at[i], qr_r.at[i], at_z(2 * sign))

    def q_cross(dz):
        slot = q_slot(dz)
        i = dz + 3
        return send(qbuf.at[slot], qbuf.at[slot], qx_s.at[i], qx_r.at[i], at_z(0, xl=1 - x_lo))

    def p_core(dy, chunk):
        slot = p_slot(dy, chunk)
        i = len(c_copies)
        c_copies.append(send(pbuf.at[slot], pbuf.at[slot], pc_s.at[i], pc_r.at[i], at_y(0, c=1 - core)))

    far = (4, 3, -3)
    p_x = {}

    def p_cross(dy):
        slot, i = p_slot(dy, 0), (far + (0,)).index(dy)
        p_x[dy] = send(pbuf.at[slot], pbuf.at[slot], px_s.at[i], px_r.at[i], at_y(0, xh=1 - x_hi))

    q_in, x_in, p_in = {}, [], {}
    for step in (2, -2, 1, -1):
        q_in[step] = q_send(0, step)
    x_in.append(q_cross(0))
    p_cross(0)
    for step in (2, -2, 1, -1):
        p_in[0, step] = p_send(0, 0, step)
    p_core(0, 0)

    for c in loads:
        c.wait()

    for sign in (1, -1):
        q_in[sign].wait_recv()
        x_in.append(q_cross(-sign))
    for sign in (1, -1):
        q_in[2 * sign].wait_recv()
        q_in[3 * sign] = q_send(-2 * sign, sign)
        q_in[4 * sign] = q_half(sign)
        x_in.append(q_cross(-2 * sign))
    for sign in (1, -1):
        p_in[0, sign].wait_recv()
        p_core(-sign, 0)

    def p_second(chunk):
        for sign in (1, -1):
            p_in[chunk, 2 * sign].wait_recv()
            if chunk == 0:
                p_in[0, 3 * sign] = p_send(0, -2 * sign, sign)
                p_in[0, 4 * sign] = p_half(0, sign)
            p_core(-2 * sign, chunk)

    def p_third():
        for sign in (1, -1):
            p_in[0, 3 * sign].wait_recv()
            p_cross(-3 * sign)
            p_core(-3 * sign, 0)
        for sign in (1, -1):
            p_in[0, 4 * sign].wait_recv()
        p_cross(4)
        p_core(4, 0)

    def p_last():
        for dy in (-3, 3, 4):
            p_x[dy].wait_recv()
            p_core(dy, 1)

    p_second(0)
    p_x[0].wait_recv()
    for step in (2, -2, 1, -1):
        p_in[1, step] = p_send(1, 0, step)
    p_core(0, 1)
    for sign in (1, -1):
        q_in[3 * sign].wait_recv()
        x_in.append(q_cross(-3 * sign))
    for sign in (1, -1):
        q_in[4 * sign].wait_recv()
    x_in.append(q_cross(4))
    p_third()
    for sign in (1, -1):
        p_in[1, sign].wait_recv()
        p_core(-sign, 1)
    p_second(1)

    for c in x_in:
        c.wait_recv()
    q_all = qbuf[...].reshape(L, L)
    for t in range(2):
        mix[t] = nt(cross[t, 0], q_all).astype(BF16)
    for t in range(2):
        d = nt(cot[t, 0], mix[t]).astype(BF16)
        for s in range(32):
            dpart[s % 2, s // 4, (s // 2) % 2, t] = d[s * 16:(s + 1) * 16]

    order = (4, 3, -3, 2, -2, 1, -1, 0)
    d_in = {}
    for i, dy in enumerate(order):
        dest = (y + dy + RING) % RING
        d_in[dy] = send(
            dpart.at[1 - core, dest], dcore.at[dest], dc_s.at[i], dc_r.at[i], at_y(0, c=1 - core)
        )

    e_in = {}

    def d_local(dy, chunk):
        dest = (y + dy + RING) % RING
        xh = x_hi if chunk == 0 else 1 - x_hi
        return dpart[core, dest, xh].astype(F32) + dcore[dest, xh].astype(F32)

    def e_local(dz):
        return epart[q_slot(dz)].astype(F32) + ecross[order.index(dz)].astype(F32)

    d_out, e_out = {}, {}

    def d_send(chunk, dy, step, value):
        i = place(chunk, dy)
        dstage[i] = value.astype(BF16)
        d_out[chunk, dy] = send(dstage.at[i], drecv.at[i], dr_s.at[i], dr_r.at[i], at_y(step))

    def d_half(chunk, sign):
        h = (1 - sign) // 2
        i, j = place(chunk, 4), place(chunk, 4, h)
        d_out[chunk, 4 * sign] = send(
            dstage.at[i, h], drecv.at[i, h], dr_s.at[j], dr_r.at[j], at_y(2 * sign)
        )

    def e_send(dz, step, value):
        i = place(0, dz)
        estage[i] = value.astype(BF16)
        e_out[dz] = send(estage.at[i], erecv.at[i], er_s.at[i], er_r.at[i], at_z(step))

    def e_half(sign):
        h = (1 - sign) // 2
        i, j = place(0, 4), place(0, 4, h)
        rows = pl.ds(h * 16, 16)
        e_out[4 * sign] = send(
            estage.at[i, rows], erecv.at[i, rows], er_s.at[j], er_r.at[j], at_z(2 * sign)
        )

    d_x = {}

    def d_cross():
        for i, dy in enumerate(far):
            dxs[i] = d_local(dy, 1).astype(BF16)
            d_x[dy] = send(dxs.at[i], dcross.at[i], dx_s.at[i], dx_r.at[i], at_y(0, xh=1 - x_hi))
        for step in (2, -2, 1, -1):
            d_send(1, step, step, d_local(step, 1))

    def d_far(dy):
        d_x[dy].wait_recv()
        return d_local(dy, 0) + dcross[far.index(dy)].astype(F32)

    def d_first(chunk):
        dstage[place(chunk, 4)] = d_far(4).astype(BF16)
        for sign in (1, -1):
            d_half(chunk, sign)
        for sign in (1, -1):
            d_send(chunk, 3 * sign, sign, d_far(3 * sign))

    def d_second(chunk):
        for sign in (1, -1):
            d_out[chunk, 3 * sign].wait_recv()
            d_out[chunk, 4 * sign].wait_recv()
            h = (1 - sign) // 2
            total = d_local(2 * sign, chunk) + drecv[place(chunk, 3 * sign)].astype(F32)
            far = drecv[place(chunk, 4), h].astype(F32)
            both = [total[0], total[1]]
            both[h] = both[h] + far
            i = place(chunk, 2 * sign)
            dstage[i, 0] = both[0].astype(BF16)
            dstage[i, 1] = both[1].astype(BF16)
            d_out[chunk, 2 * sign] = send(dstage.at[i], drecv.at[i], dr_s.at[i], dr_r.at[i], at_y(2 * sign))

    def d_third(chunk):
        for sign in (1, -1):
            d_send(chunk, sign, sign, d_local(sign, chunk))

    def e_first():
        for dz in (4, 3, -3):
            e_in[dz].wait_recv()
        estage[place(0, 4)] = e_local(4).astype(BF16)
        for sign in (1, -1):
            e_half(sign)
        for sign in (1, -1):
            e_send(3 * sign, sign, e_local(3 * sign))

    def e_second():
        for dz in (2, -2):
            e_in[dz].wait_recv()
        for sign in (1, -1):
            e_out[3 * sign].wait_recv()
            e_out[4 * sign].wait_recv()
            h = (1 - sign) // 2
            total = e_local(2 * sign) + erecv[place(0, 3 * sign)].astype(F32)
            far = erecv[place(0, 4), h * 16:(h + 1) * 16].astype(F32)
            both = [total[:16], total[16:]]
            both[h] = both[h] + far
            i = place(0, 2 * sign)
            estage[i, 0:16] = both[0].astype(BF16)
            estage[i, 16:32] = both[1].astype(BF16)
            e_out[2 * sign] = send(estage.at[i], erecv.at[i], er_s.at[i], er_r.at[i], at_z(2 * sign))

    def e_third():
        for dz in (1, -1, 0):
            e_in[dz].wait_recv()
        for sign in (1, -1):
            e_send(sign, sign, e_local(sign))

    for dy in order:
        d_in[dy].wait_recv()
    d_cross()
    p_last()
    for c in c_copies:
        c.wait_recv()
    for t in range(2):
        p_t = pbuf[:, t].reshape(L, L)
        left[t] = nn(p_t, cross[t, 0]).astype(BF16)
    e = tn(cot[0, 0], left[0]) + tn(cot[1, 0], left[1])
    epart[...] = e.astype(BF16).reshape(16, 32, L)

    for i, dz in enumerate(order):
        slot = q_slot(dz, 1)
        e_in[dz] = send(epart.at[slot], ecross.at[i], ex_s.at[i], ex_r.at[i], at_z(0, xl=1 - x_lo))

    def out_part(t):
        outv[t, 0] = nn(pbuf[:, t].reshape(L, L), mix[t]).astype(BF16)

    def held_part(t):
        held[t] = nn(cot[t, 0], qbuf[...].reshape(L, L)).astype(BF16)

    def gcross_part(t):
        gcv[t, 0] = tn(pbuf[:, t].reshape(L, L), held[t]).astype(BF16)

    def d_final(chunk):
        total = d_local(0, chunk)
        for step in (1, -1, 2, -2):
            d_out[chunk, step].wait_recv()
            total += drecv[place(chunk, step)].astype(F32)
        return total

    d_first(0)
    held_part(0)
    e_first()
    held_part(1)
    d_third(0)
    dlast[0] = d_final(1).astype(BF16)
    dx = send(dlast.at[0], dlast.at[1], dx_s.at[3], dx_r.at[3], at_y(0, xh=1 - x_hi))
    out_part(0)
    d_second(0)
    e_second()
    e_third()
    out_part(1)
    gcross_part(0)
    gcross_part(1)
    d_own = d_final(0)
    dx.wait_recv()
    gtgt_ref[...] = soft_back(pbuf[s_id], d_own + dlast[1].astype(F32))
    total = e_local(0)
    for step in (1, -1, 2, -2):
        e_out[step].wait_recv()
        total += erecv[place(0, step)].astype(F32)
    gsup_ref[0] = soft_back(qbuf[t_id], total)

    for copy in pending:
        copy.wait_send()


def write_out(*refs):
    copies = [pltpu.make_async_copy(refs[i], refs[4 + i], refs[8].at[i]) for i in range(4)]
    for copy in copies:
        copy.start()
    for copy in copies:
        copy.wait()


def body(cross_kernel, cotangent, self_tgt, self_sup):
    vmem, dma = pltpu.VMEM, pltpu.SemaphoreType.DMA
    hbm_spec = pl.BlockSpec(memory_space=pltpu.HBM)
    vmem_spec = pl.BlockSpec(memory_space=pltpu.VMEM)
    docs = (2, 1, L, L)
    outs = (
        jax.ShapeDtypeStruct(docs, BF16),
        jax.ShapeDtypeStruct(docs, BF16),
        jax.ShapeDtypeStruct((2, 16, L), F32),
        jax.ShapeDtypeStruct((1, 32, L), F32),
    )
    results = pl.pallas_call(
        kernel,
        out_shape=outs,
        in_specs=[hbm_spec] * 4,
        out_specs=(vmem_spec,) * 4,
        scratch_shapes=[
            vmem(docs, BF16), vmem(docs, BF16), vmem((2, 16, L), BF16), vmem((1, 32, L), BF16),
            vmem((32, 2, 16, L), BF16), vmem((16, 32, L), BF16),
            vmem((2, L, L), BF16), vmem((2, L, L), BF16), vmem((2, L, L), BF16),
            vmem((2, 8, 2, 2, 16, L), BF16), vmem((8, 2, 2, 16, L), BF16),
            vmem((16, 32, L), BF16), vmem((8, 32, L), BF16),
            vmem((18, 2, 16, L), BF16), vmem((18, 2, 16, L), BF16),
            vmem((9, 32, L), BF16), vmem((9, 32, L), BF16),
            vmem((2, 2, 16, L), BF16), vmem((3, 2, 16, L), BF16), vmem((3, 2, 16, L), BF16),
            dma((4,)),
            dma((4,)), dma((4,)), dma((8,)), dma((8,)), dma((18,)), dma((18,)), dma((9,)), dma((9,)), dma((16,)), dma((16,)),
            dma((8,)), dma((8,)), dma((18,)), dma((18,)), dma((9,)), dma((9,)), dma((4,)), dma((4,)), dma((8,)), dma((8,)),
        ],
        compiler_params=pltpu.CompilerParams(
            collective_id=0, has_side_effects=True, vmem_limit_bytes=48 * 1024 * 1024
        ),
        name="layer",
    )(*[pltpu.with_memory_space_constraint(x, pltpu.HBM) for x in (cross_kernel, cotangent, self_tgt, self_sup)])
    return pl.pallas_call(
        write_out,
        out_shape=outs,
        in_specs=[vmem_spec] * 4,
        out_specs=(hbm_spec,) * 4,
        scratch_shapes=[dma((4,))],
        compiler_params=pltpu.CompilerParams(vmem_limit_bytes=1024 * 1024),
        name="write_out",
    )(*results)


def solution(mesh):
    in_specs = (
        P("tgt", "sup", None, None),
        P("tgt", "sup", None, None),
        P("tgt", "sup", None),
        P("sup", "tgt", None),
    )
    out_specs = (
        P("tgt", "sup", None, None),
        P("tgt", "sup", None, None),
        P("tgt", "sup", None),
        P("sup", "tgt", None),
    )
    return jax.shard_map(body, mesh=mesh, in_specs=in_specs, out_specs=out_specs, check_vma=False)
```

```python
import jax
import jax.numpy as jnp
from jax import lax
from jax.experimental import pallas as pl
from jax.experimental.pallas import tpu as pltpu
from jax.sharding import PartitionSpec as P

MESH = pl.DeviceIdType.MESH
F32 = jnp.float32
BF16 = jnp.bfloat16
L = 512
RING = 8


def softmax_rows(scores):
    scores = scores.astype(F32)
    e = jnp.exp(scores - jnp.max(scores, axis=-1, keepdims=True))
    return (e / jnp.sum(e, axis=-1, keepdims=True)).astype(BF16)


def soft_back(probs, dprobs):
    weights = probs.astype(F32)
    return weights * (dprobs - jnp.sum(dprobs * weights, axis=-1, keepdims=True))


def nn(a, b):
    return lax.dot_general(a, b, (((1,), (0,)), ((), ())), preferred_element_type=F32)


def nt(a, b):
    return lax.dot_general(a, b, (((1,), (1,)), ((), ())), preferred_element_type=F32)


def tn(a, b):
    return lax.dot_general(a, b, (((0,), (0,)), ((), ())), preferred_element_type=F32)


def kernel(
    cross_hbm, cot_hbm, tgt_hbm, sup_hbm,
    outv, gcv, gtgt_ref, gsup_ref,
    cross, cot, tgt_ref, sup_ref, pbuf, qbuf, mix, held, left,
    dpart, dcore, epart, ecross, dstage, drecv, estage, erecv, dlast, dxs, dcross,
    load_sem,
    px_s, px_r, qx_s, qx_r, pr_s, pr_r, qr_s, qr_r, pc_s, pc_r,
    dc_s, dc_r, dr_s, dr_r, er_s, er_r, dx_s, dx_r, ex_s, ex_r,
):
    t_id = lax.axis_index("tgt")
    s_id = lax.axis_index("sup")
    z, x_lo = t_id // 2, t_id % 2
    y, x_hi, core = s_id // 4, (s_id // 2) % 2, s_id % 2

    def at_y(dy, xh=None, c=None):
        xh = x_hi if xh is None else xh
        c = core if c is None else c
        return (t_id, ((y + dy + RING) % RING) * 4 + xh * 2 + c)

    def at_z(dz, xl=None):
        xl = x_lo if xl is None else xl
        return (((z + dz + RING) % RING) * 2 + xl, s_id)

    loads = [
        pltpu.make_async_copy(tgt_hbm, tgt_ref, load_sem.at[2]),
        pltpu.make_async_copy(sup_hbm, sup_ref, load_sem.at[3]),
        pltpu.make_async_copy(cross_hbm, cross, load_sem.at[0]),
        pltpu.make_async_copy(cot_hbm, cot, load_sem.at[1]),
    ]
    for c in loads:
        c.start()

    barrier = pltpu.get_barrier_semaphore()
    near = [at_y(0, xh=1 - x_hi), at_y(0, c=1 - core), at_z(0, xl=1 - x_lo)]
    near += [at(step) for at in (at_y, at_z) for step in (2, -2, 1, -1)]
    for device in near:
        pl.semaphore_signal(barrier, inc=1, device_id=device, device_id_type=MESH)

    loads.pop(0).wait()
    loads.pop(0).wait()
    p_own = softmax_rows(tgt_ref[...])
    q_own = softmax_rows(sup_ref[0])
    pbuf[s_id] = p_own
    qbuf[t_id] = q_own
    pl.semaphore_wait(barrier, len(near))

    pending = []

    def send(src, dst, ssem, rsem, device):
        copy = pltpu.make_async_remote_copy(
            src_ref=src, dst_ref=dst, send_sem=ssem, recv_sem=rsem, device_id=device, device_id_type=MESH
        )
        copy.start()
        pending.append(copy)
        return copy

    def p_slot(dy, chunk):
        xh = x_hi if chunk == 0 else 1 - x_hi
        return ((y + dy + RING) % RING) * 4 + xh * 2 + core

    def q_slot(dz, chunk=0):
        xl = x_lo if chunk == 0 else 1 - x_lo
        return ((z + dz + RING) % RING) * 2 + xl

    def place(chunk, origin, half=0):
        return chunk * 9 + (origin + 3 if origin != 4 else 7 + half)

    c_copies = []

    def p_send(chunk, origin, step):
        slot = p_slot(origin, chunk)
        i = place(chunk, origin - step)
        return send(pbuf.at[slot], pbuf.at[slot], pr_s.at[i], pr_r.at[i], at_y(step))

    def p_half(chunk, sign):
        slot = p_slot(-2 * sign, chunk)
        h = (1 - sign) // 2
        i = place(chunk, 4, h)
        return send(pbuf.at[slot, h], pbuf.at[slot, h], pr_s.at[i], pr_r.at[i], at_y(2 * sign))

    def q_send(origin, step):
        slot = q_slot(origin)
        i = place(0, origin - step)
        return send(qbuf.at[slot], qbuf.at[slot], qr_s.at[i], qr_r.at[i], at_z(step))

    def q_half(sign):
        slot = q_slot(-2 * sign)
        h = (1 - sign) // 2
        i = place(0, 4, h)
        rows = pl.ds(h * 16, 16)
        return send(qbuf.at[slot, rows], qbuf.at[slot, rows], qr_s.at[i], qr_r.at[i], at_z(2 * sign))

    def q_cross(dz):
        slot = q_slot(dz)
        i = dz + 3
        return send(qbuf.at[slot], qbuf.at[slot], qx_s.at[i], qx_r.at[i], at_z(0, xl=1 - x_lo))

    def p_core(dy, chunk):
        slot = p_slot(dy, chunk)
        i = len(c_copies)
        c_copies.append(send(pbuf.at[slot], pbuf.at[slot], pc_s.at[i], pc_r.at[i], at_y(0, c=1 - core)))

    far = (4, 3, -3)
    p_x = {}

    def p_cross(dy):
        slot, i = p_slot(dy, 0), (far + (0,)).index(dy)
        p_x[dy] = send(pbuf.at[slot], pbuf.at[slot], px_s.at[i], px_r.at[i], at_y(0, xh=1 - x_hi))

    q_in, x_in, p_in = {}, [], {}
    for step in (2, -2, 1, -1):
        q_in[step] = q_send(0, step)
    x_in.append(q_cross(0))
    p_cross(0)
    for step in (2, -2, 1, -1):
        p_in[0, step] = p_send(0, 0, step)
    p_core(0, 0)

    for c in loads:
        c.wait()

    for sign in (1, -1):
        q_in[sign].wait_recv()
        x_in.append(q_cross(-sign))
    for sign in (1, -1):
        q_in[2 * sign].wait_recv()
        q_in[3 * sign] = q_send(-2 * sign, sign)
        q_in[4 * sign] = q_half(sign)
        x_in.append(q_cross(-2 * sign))
    for sign in (1, -1):
        p_in[0, sign].wait_recv()
        p_core(-sign, 0)

    def p_second(chunk):
        for sign in (1, -1):
            p_in[chunk, 2 * sign].wait_recv()
            if chunk == 0:
                p_in[0, 3 * sign] = p_send(0, -2 * sign, sign)
                p_in[0, 4 * sign] = p_half(0, sign)
            p_core(-2 * sign, chunk)

    def p_third():
        for sign in (1, -1):
            p_in[0, 3 * sign].wait_recv()
            p_cross(-3 * sign)
            p_core(-3 * sign, 0)
        for sign in (1, -1):
            p_in[0, 4 * sign].wait_recv()
        p_cross(4)
        p_core(4, 0)

    def p_last():
        for dy in (-3, 3, 4):
            p_x[dy].wait_recv()
            p_core(dy, 1)

    p_second(0)
    p_x[0].wait_recv()
    for step in (2, -2, 1, -1):
        p_in[1, step] = p_send(1, 0, step)
    p_core(0, 1)
    for sign in (1, -1):
        q_in[3 * sign].wait_recv()
        x_in.append(q_cross(-3 * sign))
    for sign in (1, -1):
        q_in[4 * sign].wait_recv()
    x_in.append(q_cross(4))
    p_third()
    for sign in (1, -1):
        p_in[1, sign].wait_recv()
        p_core(-sign, 1)
    p_second(1)

    for c in x_in:
        c.wait_recv()
    q_all = qbuf[...].reshape(L, L)
    mix[...] = nt(cross[...].reshape(2 * L, L), q_all).astype(BF16).reshape(2, L, L)
    for t in range(2):
        d = nt(cot[t, 0], mix[t]).astype(BF16)
        for s in range(32):
            dpart[s % 2, s // 4, (s // 2) % 2, t] = d[s * 16:(s + 1) * 16]

    order = (4, 3, -3, 2, -2, 1, -1, 0)
    d_in = {}
    for i, dy in enumerate(order):
        dest = (y + dy + RING) % RING
        d_in[dy] = send(
            dpart.at[1 - core, dest], dcore.at[dest], dc_s.at[i], dc_r.at[i], at_y(0, c=1 - core)
        )

    e_in = {}

    def d_local(dy, chunk):
        dest = (y + dy + RING) % RING
        xh = x_hi if chunk == 0 else 1 - x_hi
        return dpart[core, dest, xh].astype(F32) + dcore[dest, xh].astype(F32)

    def e_local(dz):
        return epart[q_slot(dz)].astype(F32) + ecross[order.index(dz)].astype(F32)

    d_out, e_out = {}, {}

    def d_send(chunk, dy, step, value):
        i = place(chunk, dy)
        dstage[i] = value.astype(BF16)
        d_out[chunk, dy] = send(dstage.at[i], drecv.at[i], dr_s.at[i], dr_r.at[i], at_y(step))

    def d_half(chunk, sign):
        h = (1 - sign) // 2
        i, j = place(chunk, 4), place(chunk, 4, h)
        d_out[chunk, 4 * sign] = send(
            dstage.at[i, h], drecv.at[i, h], dr_s.at[j], dr_r.at[j], at_y(2 * sign)
        )

    def e_send(dz, step, value):
        i = place(0, dz)
        estage[i] = value.astype(BF16)
        e_out[dz] = send(estage.at[i], erecv.at[i], er_s.at[i], er_r.at[i], at_z(step))

    def e_half(sign):
        h = (1 - sign) // 2
        i, j = place(0, 4), place(0, 4, h)
        rows = pl.ds(h * 16, 16)
        e_out[4 * sign] = send(
            estage.at[i, rows], erecv.at[i, rows], er_s.at[j], er_r.at[j], at_z(2 * sign)
        )

    d_x = {}

    def d_cross():
        for i, dy in enumerate(far):
            dxs[i] = d_local(dy, 1).astype(BF16)
            d_x[dy] = send(dxs.at[i], dcross.at[i], dx_s.at[i], dx_r.at[i], at_y(0, xh=1 - x_hi))
        for step in (2, -2, 1, -1):
            d_send(1, step, step, d_local(step, 1))

    def d_far(dy):
        d_x[dy].wait_recv()
        return d_local(dy, 0) + dcross[far.index(dy)].astype(F32)

    def d_first(chunk):
        dstage[place(chunk, 4)] = d_far(4).astype(BF16)
        for sign in (1, -1):
            d_half(chunk, sign)
        for sign in (1, -1):
            d_send(chunk, 3 * sign, sign, d_far(3 * sign))

    def d_second(chunk):
        for sign in (1, -1):
            d_out[chunk, 3 * sign].wait_recv()
            d_out[chunk, 4 * sign].wait_recv()
            h = (1 - sign) // 2
            total = d_local(2 * sign, chunk) + drecv[place(chunk, 3 * sign)].astype(F32)
            far = drecv[place(chunk, 4), h].astype(F32)
            both = [total[0], total[1]]
            both[h] = both[h] + far
            i = place(chunk, 2 * sign)
            dstage[i, 0] = both[0].astype(BF16)
            dstage[i, 1] = both[1].astype(BF16)
            d_out[chunk, 2 * sign] = send(dstage.at[i], drecv.at[i], dr_s.at[i], dr_r.at[i], at_y(2 * sign))

    def d_third(chunk):
        for sign in (1, -1):
            d_send(chunk, sign, sign, d_local(sign, chunk))

    def e_first():
        for dz in (4, 3, -3):
            e_in[dz].wait_recv()
        estage[place(0, 4)] = e_local(4).astype(BF16)
        for sign in (1, -1):
            e_half(sign)
        for sign in (1, -1):
            e_send(3 * sign, sign, e_local(3 * sign))

    def e_second():
        for dz in (2, -2):
            e_in[dz].wait_recv()
        for sign in (1, -1):
            e_out[3 * sign].wait_recv()
            e_out[4 * sign].wait_recv()
            h = (1 - sign) // 2
            total = e_local(2 * sign) + erecv[place(0, 3 * sign)].astype(F32)
            far = erecv[place(0, 4), h * 16:(h + 1) * 16].astype(F32)
            both = [total[:16], total[16:]]
            both[h] = both[h] + far
            i = place(0, 2 * sign)
            estage[i, 0:16] = both[0].astype(BF16)
            estage[i, 16:32] = both[1].astype(BF16)
            e_out[2 * sign] = send(estage.at[i], erecv.at[i], er_s.at[i], er_r.at[i], at_z(2 * sign))

    def e_third():
        for dz in (1, -1, 0):
            e_in[dz].wait_recv()
        for sign in (1, -1):
            e_send(sign, sign, e_local(sign))

    for dy in order:
        d_in[dy].wait_recv()
    d_cross()
    p_last()
    for c in c_copies:
        c.wait_recv()
    for t in range(2):
        p_t = pbuf[:, t].reshape(L, L)
        left[t] = nn(p_t, cross[t, 0]).astype(BF16)
    e = tn(cot[...].reshape(2 * L, L), left[...].reshape(2 * L, L))
    epart[...] = e.astype(BF16).reshape(16, 32, L)

    for i, dz in enumerate(order):
        slot = q_slot(dz, 1)
        e_in[dz] = send(epart.at[slot], ecross.at[i], ex_s.at[i], ex_r.at[i], at_z(0, xl=1 - x_lo))

    def out_part(t):
        outv[t, 0] = nn(pbuf[:, t].reshape(L, L), mix[t]).astype(BF16)

    def held_part(t):
        held[t] = nn(cot[t, 0], qbuf[...].reshape(L, L)).astype(BF16)

    def gcross_part(t):
        gcv[t, 0] = tn(pbuf[:, t].reshape(L, L), held[t]).astype(BF16)

    def d_final(chunk):
        total = d_local(0, chunk)
        for step in (1, -1, 2, -2):
            d_out[chunk, step].wait_recv()
            total += drecv[place(chunk, step)].astype(F32)
        return total

    d_first(0)
    held_part(0)
    e_first()
    held_part(1)
    d_third(0)
    dlast[0] = d_final(1).astype(BF16)
    dx = send(dlast.at[0], dlast.at[1], dx_s.at[3], dx_r.at[3], at_y(0, xh=1 - x_hi))
    out_part(0)
    d_second(0)
    e_second()
    e_third()
    out_part(1)
    gcross_part(0)
    gcross_part(1)
    d_own = d_final(0)
    dx.wait_recv()
    gtgt_ref[...] = soft_back(pbuf[s_id], d_own + dlast[1].astype(F32))
    total = e_local(0)
    for step in (1, -1, 2, -2):
        e_out[step].wait_recv()
        total += erecv[place(0, step)].astype(F32)
    gsup_ref[0] = soft_back(qbuf[t_id], total)

    for copy in pending:
        copy.wait_send()


def write_out(*refs):
    copies = [pltpu.make_async_copy(refs[i], refs[4 + i], refs[8].at[i]) for i in range(4)]
    for copy in copies:
        copy.start()
    for copy in copies:
        copy.wait()


def body(cross_kernel, cotangent, self_tgt, self_sup):
    vmem, dma = pltpu.VMEM, pltpu.SemaphoreType.DMA
    hbm_spec = pl.BlockSpec(memory_space=pltpu.HBM)
    vmem_spec = pl.BlockSpec(memory_space=pltpu.VMEM)
    docs = (2, 1, L, L)
    outs = (
        jax.ShapeDtypeStruct(docs, BF16),
        jax.ShapeDtypeStruct(docs, BF16),
        jax.ShapeDtypeStruct((2, 16, L), F32),
        jax.ShapeDtypeStruct((1, 32, L), F32),
    )
    results = pl.pallas_call(
        kernel,
        out_shape=outs,
        in_specs=[hbm_spec] * 4,
        out_specs=(vmem_spec,) * 4,
        scratch_shapes=[
            vmem(docs, BF16), vmem(docs, BF16), vmem((2, 16, L), BF16), vmem((1, 32, L), BF16),
            vmem((32, 2, 16, L), BF16), vmem((16, 32, L), BF16),
            vmem((2, L, L), BF16), vmem((2, L, L), BF16), vmem((2, L, L), BF16),
            vmem((2, 8, 2, 2, 16, L), BF16), vmem((8, 2, 2, 16, L), BF16),
            vmem((16, 32, L), BF16), vmem((8, 32, L), BF16),
            vmem((18, 2, 16, L), BF16), vmem((18, 2, 16, L), BF16),
            vmem((9, 32, L), BF16), vmem((9, 32, L), BF16),
            vmem((2, 2, 16, L), BF16), vmem((3, 2, 16, L), BF16), vmem((3, 2, 16, L), BF16),
            dma((4,)),
            dma((4,)), dma((4,)), dma((8,)), dma((8,)), dma((18,)), dma((18,)), dma((9,)), dma((9,)), dma((16,)), dma((16,)),
            dma((8,)), dma((8,)), dma((18,)), dma((18,)), dma((9,)), dma((9,)), dma((4,)), dma((4,)), dma((8,)), dma((8,)),
        ],
        compiler_params=pltpu.CompilerParams(
            collective_id=0, has_side_effects=True, vmem_limit_bytes=48 * 1024 * 1024
        ),
        name="layer",
    )(*[pltpu.with_memory_space_constraint(x, pltpu.HBM) for x in (cross_kernel, cotangent, self_tgt, self_sup)])
    return pl.pallas_call(
        write_out,
        out_shape=outs,
        in_specs=[vmem_spec] * 4,
        out_specs=(hbm_spec,) * 4,
        scratch_shapes=[dma((4,))],
        compiler_params=pltpu.CompilerParams(vmem_limit_bytes=1024 * 1024),
        name="write_out",
    )(*results)


def solution(mesh):
    in_specs = (
        P("tgt", "sup", None, None),
        P("tgt", "sup", None, None),
        P("tgt", "sup", None),
        P("sup", "tgt", None),
    )
    out_specs = (
        P("tgt", "sup", None, None),
        P("tgt", "sup", None, None),
        P("tgt", "sup", None),
        P("sup", "tgt", None),
    )
    return jax.shard_map(body, mesh=mesh, in_specs=in_specs, out_specs=out_specs, check_vma=False)
```
